32 devices in a mesh: groups: 2 (over y), blk: 4 (over z), head: 2 (over x), sub: 2 (over core).
Axes of the slice: x: 2, y: 2, z: 4, core: 2. Of those that a mesh axis runs over, the one named last changes fastest.
Arguments:
- queries: bfloat16 [128, 32, 128], P(('groups', 'blk'), ('head', 'sub')), parts along dimension 0, may hold values from -16 to 16
- key_cache: bfloat16 [2, 128, 256, 128], P('head', ('groups', 'blk')), parts along dimension 1, may hold values from -8 to 8
- cached_value_slots: bfloat16 [2, 128, 256, 128], P('head', ('groups', 'blk')), parts along dimension 1, may hold values from -6 to 6
- block_counts: int32 [8], P('groups'), parts along dimension 0, may hold values from 2 to 16, as said below
- slot_blocks: int32 [128], P('groups'), parts along dimension 0, may hold values from -1 to 31, as said below
- offsets: int32 [128], P('groups'), parts along dimension 0, may hold values from 4096 to 8192
Outputs:
- attended: bfloat16 [128, 32, 128], P(('groups', 'blk'), ('head', 'sub')), parts along dimension 0
The draws below stay inside these ranges and needn't reach their ends.
There are 2 independent parts, one for each index of `groups`. The reference program is written for one: setup_inputs(seed, part) draws one part's arguments, and reference() takes and returns one part's arrays. A program takes and returns all parts, laid end to end along the dimension named above; each array names one. Nothing has to cross between parts.
Inputs may be any that keep to these rules, and one draw needn't show every extreme that they name: block_counts[i] is the number of live slots of index i of blk; the counts sum to 32. `slot_blocks`: entry i * 16 + s holds a block number when s < block_counts[i] and -1 otherwise; every block number below 32 stands in exactly one live slot.
All inputs are finite; a program needn't handle non-finite values.
Results may differ from the reference program's by a relative error of at most 0.0065.
Values may be sent and summed in bfloat16 or wider, within the bound.
No kernel may reach another device: no remote copies, remote signals or barrier semaphores. Data moves between devices by JAX's collectives and lax.ppermute only.
A program may use at most 64 MiB of HBM per device.

```python
import jax
import jax.numpy as jnp
from jax import lax

HEAD_SIZE = 128
GROUP = 16
BLOCK_POSITIONS = 256
CAP = 16
KEY_VALUE_HEADS = 2
QH = 32
Q = 64
SLOT_COUNT = 64
CTX = 8192
N_BLK = 4


def layout_tables(key):
    base_key = jax.random.fold_in(key, 21)
    half_members = N_BLK // 2
    pair_order = jax.random.permutation(jax.random.fold_in(base_key, 1), half_members)
    pair_side = jax.random.randint(jax.random.fold_in(base_key, 4), (half_members,), 0, 2)
    mean_blocks = CAP // 2
    spread = jax.random.randint(jax.random.fold_in(base_key, 2), (N_BLK,), 0, mean_blocks - 1)
    position = jnp.arange(N_BLK)
    pair_index = jnp.clip((position - 4) // 2, 0, N_BLK - 1)
    pair_sign = jnp.where((position - 4) % 2 == 0, 1, -1)
    shifted = jnp.where(position == 0, mean_blocks, jnp.where(position == 1, 2 - mean_blocks, jnp.where(position == 2, -2, jnp.where(position == 3, 0, pair_sign * spread[pair_index]))))
    which_pair = position // 2
    which_side = jnp.bitwise_xor(position % 2, pair_side[which_pair])
    member_of = pair_order[which_pair] + half_members * which_side
    counts = jnp.zeros((N_BLK,), jnp.int32).at[member_of].set((mean_blocks + shifted).astype(jnp.int32))
    total_blocks = N_BLK * mean_blocks
    shuffled = jax.random.permutation(jax.random.fold_in(base_key, 3), total_blocks)
    starts = jnp.cumsum(counts) - counts
    block_slot_index = jnp.arange(CAP)
    flat_index = starts[:, None] + block_slot_index[None, :]
    block_ids = jnp.where(block_slot_index[None, :] < counts[:, None], shuffled[jnp.clip(flat_index, 0, total_blocks - 1)], -1)
    return (counts.astype(jnp.int32), block_ids.reshape(N_BLK * CAP).astype(jnp.int32))


def draw_block_counts(key, part):
    return layout_tables(key)[0]


def draw_slot_blocks(key, part):
    return layout_tables(key)[1]


def draw_offsets(key, part):
    limits = jax.random.randint(jax.random.fold_in(key, 41), (Q,), CTX // 2, CTX + 1)
    first = jax.random.randint(jax.random.fold_in(key, 42), (), 0, Q)
    second = (first + 1 + jax.random.randint(jax.random.fold_in(key, 43), (), 0, Q - 1)) % Q
    limits = limits.at[first].set(CTX)
    limits = limits.at[second].set(CTX // 2)
    return limits.astype(jnp.int32)


def draw_queries(key, part):
    sampled_draw = jax.random.normal(jax.random.fold_in(key, 31), (Q, QH, HEAD_SIZE), jnp.float32) * 2.5
    return jnp.clip(sampled_draw, -16.0, 16.0).astype(jnp.bfloat16)


def draw_key_cache(key, part):
    sampled_draw = jnp.clip(jax.random.normal(jax.random.fold_in(key, 51), (KEY_VALUE_HEADS, SLOT_COUNT, BLOCK_POSITIONS, HEAD_SIZE), jnp.float32), -8.0, 8.0)
    return sampled_draw.astype(jnp.bfloat16)


def levels(stream_key, dims, cuts, low, high):
    loudness = 1.0
    for dim, shards_of in cuts:
        heights = jax.random.uniform(jax.random.fold_in(jax.random.fold_in(stream_key, 6), dim), (shards_of,), jnp.float32, low / len(cuts), high / len(cuts))
        loudness = loudness * jnp.repeat(jnp.exp(heights), dims[dim] // shards_of).reshape((-1,) + (1,) * (len(dims) - 1 - dim))
    return loudness


def noise(rng, extent, deviation, limit, split=(), held_as=jnp.bfloat16):
    entries = deviation * jax.random.normal(rng, extent, jnp.float32)
    if split:
        entries = entries * levels(rng, extent, split, -0.22, 0.18)
    return jnp.clip(entries, -limit, limit).astype(held_as)


def setup_inputs(seed: int = 0, part: int = 0) -> dict:
    key_of = jax.random.split(jax.random.key(seed), 7)
    own_keys = jax.random.split(jax.random.fold_in(key_of[6], part), 7)
    return {
        "queries": draw_queries(jax.random.fold_in(jax.random.fold_in(key_of[6], part), 71), part),
        "key_cache": draw_key_cache(jax.random.fold_in(jax.random.fold_in(key_of[6], part), 71), part),
        "cached_value_slots": noise(own_keys[2], (KEY_VALUE_HEADS, SLOT_COUNT, BLOCK_POSITIONS, HEAD_SIZE), 1.0, 6.0, ((0, 2), (1, 4))),
        "block_counts": draw_block_counts(jax.random.fold_in(jax.random.fold_in(key_of[6], part), 71), part),
        "slot_blocks": draw_slot_blocks(jax.random.fold_in(jax.random.fold_in(key_of[6], part), 71), part),
        "offsets": draw_offsets(jax.random.fold_in(jax.random.fold_in(key_of[6], part), 71), part),
    }


lowest_score = -1e30


def block_update(running, q_rows, row_limit, key_block, value_block, block_id):
    row_max, row_sum, row_out = running
    scores = jnp.dot(q_rows, key_block.T, preferred_element_type=jnp.float32) * (HEAD_SIZE ** -0.5)
    position = block_id * BLOCK_POSITIONS + jnp.arange(BLOCK_POSITIONS, dtype=jnp.int32)
    visible = position[None, :] < row_limit[:, None]
    scores = jnp.where(visible, scores, lowest_score)
    new_max = jnp.maximum(row_max, jnp.max(scores, axis=1))
    weights = jnp.where(visible, jnp.exp(scores - new_max[:, None]), 0.0)
    factor = jnp.exp(row_max - new_max)
    new_sum = row_sum * factor + jnp.sum(weights, axis=1)
    new_out = row_out * factor[:, None] + jnp.dot(weights.astype(jnp.bfloat16), value_block, preferred_element_type=jnp.float32)
    return (new_max, new_sum, new_out)


def reference(queries, key_cache, cached_value_slots, block_counts, slot_blocks, offsets):
    block_slot_index = jnp.arange(SLOT_COUNT, dtype=jnp.int32)
    member = (block_slot_index // CAP).astype(jnp.int32)
    live_slot = (block_slot_index % CAP) < block_counts[member]
    q_heads = queries.reshape(Q, KEY_VALUE_HEADS, GROUP, HEAD_SIZE).transpose(1, 0, 2, 3).reshape(KEY_VALUE_HEADS, Q * GROUP, HEAD_SIZE)
    row_limit = jnp.repeat(offsets, GROUP)

    def one_head(head_args):
        q_rows, key_slots, value_slots = head_args
        initial = (jnp.full((Q * GROUP,), lowest_score, jnp.float32),
                   jnp.zeros((Q * GROUP,), jnp.float32),
                   jnp.zeros((Q * GROUP, HEAD_SIZE), jnp.float32))

        def scan_slot(running, slot_args):
            key_block, value_block, block_id, live = slot_args
            updated = lax.cond(live,
                               lambda carried: block_update(carried, q_rows, row_limit, key_block, value_block, block_id),
                               lambda carried: carried,
                               running)
            return updated, None

        final, _ = lax.scan(scan_slot, initial, (key_slots, value_slots, slot_blocks, live_slot))
        return final[2] / final[1][:, None]

    attended = lax.map(one_head, (q_heads, key_cache, cached_value_slots))
    return attended.reshape(KEY_VALUE_HEADS, Q, GROUP, HEAD_SIZE).transpose(1, 0, 2, 3).reshape(Q, QH, HEAD_SIZE).astype(jnp.bfloat16)
```

```python
import functools

import jax
import jax.numpy as jnp
from jax import lax
from jax.experimental import pallas as pl
from jax.experimental.pallas import tpu as pltpu
from jax.sharding import PartitionSpec as P

masked_score = -1e30
lowest_max = -1e29
stat_rows = 16
tile_blocks = 2
log2_e = 1.4426950408889634


def split_three(x):
    high = x.astype(jnp.bfloat16)
    rest = x - high.astype(jnp.float32)
    middle = rest.astype(jnp.bfloat16)
    low = (rest - middle.astype(jnp.float32)).astype(jnp.bfloat16)
    return high, middle, low


def attend_kernel(
    sources, counts_ref, blocks_ref, offsets_ref, *refs
):
    n = len(sources)
    q_refs, (k_ref, v_ref), out_refs = refs[:n], refs[n : n + 2], refs[n + 2 : 2 * n + 2]
    score_ref, limit_ref, sum_ref = refs[2 * n + 2 :]
    rows, width = q_refs[0].shape
    slots, block_len, _ = k_ref.shape
    tokens = offsets_ref.shape[0] // lax.axis_size("blk")
    heads = rows // tokens
    member = lax.axis_index("blk")
    members = lax.axis_size("blk")
    count = counts_ref[member]
    tiles = (count + tile_blocks - 1) // tile_blocks
    scale = width ** (-0.5) * log2_e
    lanes = 128
    tile_len = tile_blocks * block_len

    least = offsets_ref[0] * 0 + 2**30
    for part, shift in enumerate(sources):
        home = lax.rem(member + members - shift, members)
        for t in range(tokens):
            limit = offsets_ref[home * tokens + t]
            least = jnp.minimum(least, limit)
            limit_ref[part, t * heads : (t + 1) * heads, :] = jnp.full((heads, lanes), limit, jnp.int32)

    def first_of(slot):
        live = slot < count
        index = blocks_ref[member * slots + slot]
        return jnp.where(live, index * block_len, 2**30)

    lane = lax.broadcasted_iota(jnp.int32, (rows, lanes), 1)

    def score_tile(tile, tops):
        slot = tile * tile_blocks
        firsts = [first_of(slot + i) for i in range(tile_blocks)]
        last = firsts[0]
        for first in firsts[1:]:
            last = jnp.maximum(last, first)

        def tile_scores(part, i):
            return lax.dot_general(
                q_refs[part][...],
                k_ref[slot + i],
                (((1,), (1,)), ((), ())),
                preferred_element_type=jnp.float32,
            )

        def plain(tops):
            out = []
            for part in range(n):
                top = tops[part]
                for i in range(tile_blocks):
                    s = tile_scores(part, i)
                    score_ref[part, tile, :, i * block_len : (i + 1) * block_len] = s
                    for c in range(0, block_len, lanes):
                        top = jnp.maximum(top, s[:, c : c + lanes])
                out.append(top)
            return tuple(out)

        def masking(tops):
            out = []
            for part in range(n):
                top = tops[part]
                for i in range(tile_blocks):
                    s = tile_scores(part, i)
                    for c in range(0, block_len, lanes):
                        seen = lane < limit_ref[part] - (firsts[i] + c)
                        piece = jnp.where(seen, s[:, c : c + lanes], masked_score)
                        at = i * block_len + c
                        score_ref[part, tile, :, at : at + lanes] = piece
                        top = jnp.maximum(top, piece)
                out.append(top)
            return tuple(out)

        return lax.cond(last + block_len <= least, plain, masking, tops)

    tops = tuple(jnp.full((rows, lanes), lowest_max, jnp.float32) for _ in range(n))
    tops = lax.fori_loop(0, tiles, score_tile, tops)
    tops = [jnp.max(top, axis=1, keepdims=True) * scale for top in tops]

    def value_tile(tile, carried):
        slot = tile * tile_blocks
        values = v_ref[pl.ds(slot, tile_blocks)].reshape(tile_len, width)
        out = []
        for part in range(n):
            total, summed = carried[part]
            weights = jnp.exp2(score_ref[part, tile] * scale - tops[part])
            for c in range(0, tile_len, lanes):
                total = total + weights[:, c : c + lanes]
            summed = summed + jnp.dot(
                weights.astype(jnp.bfloat16), values, preferred_element_type=jnp.float32
            )
            out.append((total, summed))
        return tuple(out)

    zero = jnp.zeros((rows, lanes), jnp.float32)
    zero_out = jnp.zeros((rows, width), jnp.float32)
    carried = lax.fori_loop(0, tiles, value_tile, tuple((zero, zero_out) for _ in range(n)))
    for part in range(n):
        total = jnp.sum(carried[part][0], axis=1, keepdims=True)
        empty = total <= 0.0
        safe = jnp.where(empty, 1.0, total)
        out_refs[part][:rows, :] = (carried[part][1] / safe).astype(jnp.bfloat16)
        level = jnp.where(empty, masked_score, tops[part] + jnp.log2(safe))
        levels = jnp.transpose(jnp.broadcast_to(level, (rows, lanes)))[:stat_rows]
        high, middle, low = split_three(levels)
        row = lax.broadcasted_iota(jnp.int32, levels.shape, 0)
        packed = jnp.where(
            row == 0,
            high.astype(jnp.float32),
            jnp.where(row == 1, middle.astype(jnp.float32), low.astype(jnp.float32)),
        )
        out_refs[part][rows:, :] = packed.astype(jnp.bfloat16)


def attend(sources, queries, keys, values, counts, blocks, offsets):
    n = len(sources)
    rows, width = queries[0].shape
    slots, block_len, _ = keys.shape
    tiles = slots // tile_blocks
    smem = pl.BlockSpec(memory_space=pltpu.SMEM)
    vmem = pl.BlockSpec(memory_space=pltpu.VMEM)
    return pl.pallas_call(
        functools.partial(attend_kernel, sources),
        out_shape=[jax.ShapeDtypeStruct((rows + stat_rows, width), jnp.bfloat16)] * n,
        in_specs=[smem] * 3 + [vmem] * (n + 2),
        out_specs=[vmem] * n,
        scratch_shapes=[
            pltpu.VMEM((n, tiles, rows, tile_blocks * block_len), jnp.float32),
            pltpu.VMEM((n, rows, 128), jnp.int32),
            pltpu.VMEM((8, 128), jnp.float32),
        ],
        cost_estimate=pl.CostEstimate(
            flops=4 * n * rows * width * slots * block_len,
            bytes_accessed=4 * slots * block_len * width,
            transcendentals=n * rows * slots * block_len,
        ),
        name=f"attend_{n}",
    )(counts, blocks, offsets, *queries, keys, values)


def merge_kernel(*refs):
    parts, out_ref = refs[:-1], refs[-1]
    rows, width = out_ref.shape
    levels = []
    for part in parts:
        stats = part[rows:, :].astype(jnp.float32)
        levels.append(stats[0:1] + stats[1:2] + stats[2:3])
    top = functools.reduce(jnp.maximum, levels)
    weights = [jnp.exp2(level - top) for level in levels]
    total = functools.reduce(lambda a, b: a + b, weights)
    summed = jnp.zeros((rows, width), jnp.float32)
    for part, weight in zip(parts, weights):
        column = jnp.transpose(jnp.broadcast_to(weight / total, (width, rows)))
        summed = summed + column * part[:rows, :].astype(jnp.float32)
    out_ref[...] = summed.astype(jnp.bfloat16)


def merge(parts, rows, width):
    vmem = pl.BlockSpec(memory_space=pltpu.VMEM)
    return pl.pallas_call(
        merge_kernel,
        out_shape=jax.ShapeDtypeStruct((rows, width), jnp.bfloat16),
        in_specs=[vmem] * len(parts),
        out_specs=vmem,
        name="merge",
    )(*parts)


def shifted(x, shift):
    members = lax.axis_size("blk")
    return lax.ppermute(x, "blk", [(i, (i + shift) % members) for i in range(members)])


def per_device(queries, key_cache, cached_value_slots, block_counts, slot_blocks, offsets):
    tokens, heads, width = queries.shape
    members = lax.axis_size("blk")
    own = queries.reshape(tokens * heads, width)
    held = [own] + [shifted(own, s) for s in range(1, members)]
    parts = attend(
        tuple(range(members)),
        held,
        key_cache[0],
        cached_value_slots[0],
        block_counts,
        slot_blocks,
        offsets,
    )
    back = [parts[0]] + [shifted(parts[s], -s) for s in range(1, members)]
    return merge(back, tokens * heads, width).reshape(tokens, heads, width)


def solution(mesh):
    in_specs = (
        P(("groups", "blk"), ("head", "sub"), None),
        P("head", ("groups", "blk"), None, None),
        P("head", ("groups", "blk"), None, None),
        P("groups"),
        P("groups"),
        P("groups"),
    )
    out_specs = P(("groups", "blk"), ("head", "sub"), None)
    return jax.shard_map(
        per_device, mesh=mesh, in_specs=in_specs, out_specs=out_specs, check_vma=False
    )
```

```python
import functools

import jax
import jax.numpy as jnp
from jax import lax
from jax.experimental import pallas as pl
from jax.experimental.pallas import tpu as pltpu
from jax.sharding import PartitionSpec as P

masked_score = -1e30
lowest_max = -1e29
lanes = 128
stat_rows = 16
tile_blocks = 4
log2_e = 1.4426950408889634
far = 2**30


def split_three(x):
    high = x.astype(jnp.bfloat16)
    rest = x - high.astype(jnp.float32)
    middle = rest.astype(jnp.bfloat16)
    low = (rest - middle.astype(jnp.float32)).astype(jnp.bfloat16)
    return high.astype(jnp.float32), middle.astype(jnp.float32), low.astype(jnp.float32)


def attend_rows(
    home, counts_ref, blocks_ref, offsets_ref, q_ref, k_ref, v_ref, part_ref, score_ref, room_ref, ready
):
    rows, width = q_ref.shape
    slots, block_len, _ = k_ref.shape
    members = lax.axis_size("blk")
    member = lax.axis_index("blk")
    tokens = offsets_ref.shape[0] // members
    heads = rows // tokens
    count = counts_ref[member]
    tiles = (count + tile_blocks - 1) // tile_blocks
    scale = width ** (-0.5) * log2_e
    tile_len = tile_blocks * block_len

    lane = lax.broadcasted_iota(jnp.int32, (heads, lanes), 1)
    for t in range(tokens):
        room_ref[t * heads : (t + 1) * heads, :] = offsets_ref[home * tokens + t] - lane

    def score_tile(tile, top):
        ready(tile)
        for i in range(tile_blocks):
            slot = tile * tile_blocks + i
            first = jnp.where(slot < count, blocks_ref[member * slots + slot] * block_len, far)
            s = lax.dot_general(
                q_ref[...], k_ref[slot], (((1,), (1,)), ((), ())), preferred_element_type=jnp.float32
            )
            for c in range(0, block_len, lanes):
                piece = jnp.where(room_ref[...] > first + c, s[:, c : c + lanes], masked_score)
                at = i * block_len + c
                score_ref[tile, :, at : at + lanes] = piece
                top = jnp.maximum(top, piece)
        return top

    top = lax.fori_loop(0, tiles, score_tile, jnp.full((rows, lanes), lowest_max, jnp.float32))
    top = jnp.max(top, axis=1, keepdims=True) * scale

    def value_tile(tile, carried):
        total, summed = carried
        values = v_ref[pl.ds(tile * tile_blocks, tile_blocks)].reshape(tile_len, width)
        weights = jnp.exp2(score_ref[tile] * scale - top)
        for c in range(0, tile_len, lanes):
            total = total + weights[:, c : c + lanes]
        summed = summed + jnp.dot(
            weights.astype(jnp.bfloat16), values, preferred_element_type=jnp.float32
        )
        return total, summed

    zero = (jnp.zeros((rows, lanes), jnp.float32), jnp.zeros((rows, width), jnp.float32))
    total, summed = lax.fori_loop(0, tiles, value_tile, zero)
    total = jnp.sum(total, axis=1, keepdims=True)
    empty = total <= 0.0
    safe = jnp.where(empty, 1.0, total)
    part_ref[:rows, :] = (summed / safe).astype(jnp.bfloat16)
    level = jnp.where(empty, masked_score, top + jnp.log2(safe))
    levels = jnp.transpose(jnp.broadcast_to(level, (rows, lanes)))[:stat_rows]
    high, middle, low = split_three(levels)
    row = lax.broadcasted_iota(jnp.int32, levels.shape, 0)
    packed = jnp.where(row == 0, high, jnp.where(row == 1, middle, low))
    part_ref[rows:, :] = packed.astype(jnp.bfloat16)


def first_kernel(
    counts_ref, blocks_ref, offsets_ref, q_ref, k_hbm, v_hbm,
    part_ref, k_ref, v_ref, score_ref, room_ref, sems,
):
    member = lax.axis_index("blk")
    slots = k_ref.shape[0]
    tiles = (counts_ref[member] + tile_blocks - 1) // tile_blocks

    def copies(tile):
        here = pl.ds(tile * tile_blocks, tile_blocks)
        return (
            pltpu.make_async_copy(k_hbm.at[here], k_ref.at[here], sems.at[0, tile]),
            pltpu.make_async_copy(v_hbm.at[here], v_ref.at[here], sems.at[1, tile]),
        )

    for kind in range(2):
        for tile in range(slots // tile_blocks):

            @pl.when(tile < tiles)
            def _():
                copies(tile)[kind].start()

    def ready(tile):
        for copy in copies(tile):
            copy.wait()

    attend_rows(
        member, counts_ref, blocks_ref, offsets_ref, q_ref, k_ref, v_ref, part_ref,
        score_ref, room_ref, ready,
    )


def next_kernel(
    bit, counts_ref, blocks_ref, offsets_ref, q_ref, k_ref, v_ref, part_ref, score_ref, room_ref
):
    home = jnp.bitwise_xor(lax.axis_index("blk"), bit)
    attend_rows(
        home, counts_ref, blocks_ref, offsets_ref, q_ref, k_ref, v_ref, part_ref,
        score_ref, room_ref, lambda tile: None,
    )


def attend(bit, queries, keys, values, tables):
    rows, width = queries.shape
    slots, block_len, _ = keys.shape
    tiles = slots // tile_blocks
    smem = pl.BlockSpec(memory_space=pltpu.SMEM)
    vmem = pl.BlockSpec(memory_space=pltpu.VMEM)
    hbm = pl.BlockSpec(memory_space=pltpu.HBM)
    part = jax.ShapeDtypeStruct((rows + stat_rows, width), jnp.bfloat16)
    scratch = [
        pltpu.VMEM((tiles, rows, tile_blocks * block_len), jnp.float32),
        pltpu.VMEM((rows, lanes), jnp.int32),
    ]
    common = dict(
        cost_estimate=pl.CostEstimate(
            flops=4 * rows * width * slots * block_len,
            bytes_accessed=4 * slots * block_len * width,
            transcendentals=rows * slots * block_len,
        ),
        compiler_params=pltpu.CompilerParams(
            vmem_limit_bytes=4 * rows * slots * block_len + 8 * slots * block_len * width + 2**21
        ),
        name=f"attend_{bit}",
    )
    if bit == 0:
        return pl.pallas_call(
            first_kernel,
            out_shape=[part, keys, values],
            in_specs=[smem] * 3 + [vmem, hbm, hbm],
            out_specs=[vmem] * 3,
            scratch_shapes=scratch + [pltpu.SemaphoreType.DMA((2, tiles))],
            **common,
        )(*tables, queries, keys, values)
    return pl.pallas_call(
        functools.partial(next_kernel, bit),
        out_shape=part,
        in_specs=[smem] * 3 + [vmem] * 3,
        out_specs=vmem,
        scratch_shapes=scratch,
        **common,
    )(*tables, queries, keys, values)


def merge_kernel(*refs):
    parts, out_ref = refs[:-1], refs[-1]
    rows, width = out_ref.shape
    levels = []
    for part in parts:
        stats = part[rows:, :].astype(jnp.float32)
        levels.append(stats[0:1] + stats[1:2] + stats[2:3])
    top = functools.reduce(jnp.maximum, levels)
    weights = [jnp.exp2(level - top) for level in levels]
    total = functools.reduce(lambda a, b: a + b, weights)
    summed = jnp.zeros((rows, width), jnp.float32)
    for part, weight in zip(parts, weights):
        column = jnp.transpose(jnp.broadcast_to(weight / total, (width, rows)))
        summed = summed + column * part[:rows, :].astype(jnp.float32)
    out_ref[...] = summed.astype(jnp.bfloat16)


def merge(parts, rows, width):
    vmem = pl.BlockSpec(memory_space=pltpu.VMEM)
    return pl.pallas_call(
        merge_kernel,
        out_shape=jax.ShapeDtypeStruct((rows, width), jnp.bfloat16),
        in_specs=[vmem] * len(parts),
        out_specs=vmem,
        compiler_params=pltpu.CompilerParams(vmem_limit_bytes=2**21),
        name="merge",
    )(*parts)


def swapped(x, bit):
    return lax.ppermute(x, "blk", [(i, i ^ bit) for i in range(lax.axis_size("blk"))])


def per_device(queries, key_cache, cached_value_slots, block_counts, slot_blocks, offsets):
    tokens, heads, width = queries.shape
    members = lax.axis_size("blk")
    own = queries.reshape(tokens * heads, width)
    tables = (block_counts, slot_blocks, offsets)
    held = {bit: swapped(own, bit) for bit in range(1, members)}
    part, keys, values = attend(0, own, key_cache[0], cached_value_slots[0], tables)
    parts = [part]
    for bit in range(1, members):
        parts.append(swapped(attend(bit, held[bit], keys, values, tables), bit))
    return merge(parts, tokens * heads, width).reshape(tokens, heads, width)


def solution(mesh):
    in_specs = (
        P(("groups", "blk"), ("head", "sub"), None),
        P("head", ("groups", "blk"), None, None),
        P("head", ("groups", "blk"), None, None),
        P("groups"),
        P("groups"),
        P("groups"),
    )
    out_specs = P(("groups", "blk"), ("head", "sub"), None)
    return jax.shard_map(
        per_device, mesh=mesh, in_specs=in_specs, out_specs=out_specs, check_vma=False
    )
```

```python
import functools

import jax
import jax.numpy as jnp
from jax import lax
from jax.experimental import pallas as pl
from jax.experimental.pallas import tpu as pltpu
from jax.sharding import PartitionSpec as P

masked_score = -1e30
lowest_max = -1e29
lanes = 128
stat_rows = 16
tile_blocks = 2
group_parts = 3
log2_e = 1.4426950408889634
far = 2**30


def split_three(x):
    high = x.astype(jnp.bfloat16)
    rest = x - high.astype(jnp.float32)
    middle = rest.astype(jnp.bfloat16)
    low = (rest - middle.astype(jnp.float32)).astype(jnp.bfloat16)
    return high.astype(jnp.float32), middle.astype(jnp.float32), low.astype(jnp.float32)


def attend_rows(
    homes, counts_ref, blocks_ref, offsets_ref, q_refs, k_ref, v_ref, part_refs,
    score_ref, room_ref, q_ref, ready,
):
    every = len(homes) * q_refs[0].shape[0]
    shape = (every, 2 * q_refs[0].shape[1])
    pl.run_scoped(
        functools.partial(
            attend_scoped, homes, counts_ref, blocks_ref, offsets_ref, q_refs, k_ref, v_ref,
            part_refs, score_ref, room_ref, q_ref, ready,
        ),
        [pltpu.ACC(i % 2)(shape, jnp.float32) for i in range(tile_blocks)],
        [pltpu.ACC(i)(shape, jnp.float32) for i in range(2)],
    )


def attend_scoped(
    homes, counts_ref, blocks_ref, offsets_ref, q_refs, k_ref, v_ref, part_refs,
    score_ref, room_ref, q_ref, ready, score_accs, value_accs,
):
    rows, width = q_refs[0].shape
    slots, block_len, _ = k_ref.shape
    every = len(homes) * rows
    members = lax.axis_size("blk")
    member = lax.axis_index("blk")
    tokens = offsets_ref.shape[0] // members
    heads = rows // tokens
    count = counts_ref[member]
    tiles = (count + tile_blocks - 1) // tile_blocks
    scale = width ** (-0.5) * log2_e

    lane = lax.broadcasted_iota(jnp.int32, (heads, lanes), 1)
    for part, home in enumerate(homes):
        here = slice(part * rows, (part + 1) * rows)
        scaled = q_refs[part][...].astype(jnp.float32) * scale
        high = scaled.astype(jnp.bfloat16)
        q_ref[here, :width] = high
        q_ref[here, width:] = (scaled - high.astype(jnp.float32)).astype(jnp.bfloat16)
        for t in range(tokens):
            at = part * rows + t * heads
            room_ref[at : at + heads, :] = offsets_ref[home * tokens + t] - lane

    def score_tile(tile, top):
        ready(tile)
        for i in range(tile_blocks):
            unit = i % 2
            keys = k_ref[tile * tile_blocks + i]
            pltpu.matmul_push_rhs(
                jnp.concatenate([keys, keys], axis=1), (i // 2) % 2, unit, transpose=True
            )
            pltpu.matmul_acc_lhs(score_accs[i], q_ref[...], (i // 2) % 2)
        for i in range(tile_blocks):
            slot = tile * tile_blocks + i
            first = jnp.where(slot < count, blocks_ref[member * slots + slot] * block_len, far)
            s = pltpu.matmul_pop(score_accs[i])
            for c in range(0, block_len, lanes):
                piece = jnp.where(room_ref[...] > first + c, s[:, c : c + lanes], masked_score)
                score_ref[tile, i, :, c : c + lanes] = piece
                top = jnp.maximum(top, piece)
        return top

    top = lax.fori_loop(0, tiles, score_tile, jnp.full((every, lanes), lowest_max, jnp.float32))
    top = jnp.max(top, axis=1, keepdims=True)
    ones = jnp.ones((block_len, lanes), jnp.bfloat16)

    def value_tile(tile, carried):
        for i in range(tile_blocks):
            unit = i % 2
            values = v_ref[tile * tile_blocks + i]
            pltpu.matmul_push_rhs(jnp.concatenate([values, ones], axis=1), (i // 2) % 2, unit)
            weights = jnp.exp2(score_ref[tile, i] - top).astype(jnp.bfloat16)
            pltpu.matmul_acc_lhs(value_accs[unit], weights, (i // 2) % 2)
        return carried

    lax.fori_loop(0, tiles, value_tile, 0)
    both = pltpu.matmul_pop(value_accs[0]) + pltpu.matmul_pop(value_accs[1])
    total = both[:, width:]
    empty = total <= 0.0
    safe = jnp.where(empty, 1.0, total)
    level = jnp.where(empty, masked_score, top + jnp.log2(safe))
    summed = both[:, :width] / safe
    for part, part_ref in enumerate(part_refs):
        here = slice(part * rows, (part + 1) * rows)
        part_ref[:rows, :] = summed[here].astype(jnp.bfloat16)
        levels = jnp.transpose(level[here])[:stat_rows]
        high, middle, low = split_three(levels)
        row = lax.broadcasted_iota(jnp.int32, levels.shape, 0)
        packed = jnp.where(row == 0, high, jnp.where(row == 1, middle, low))
        part_ref[rows:, :] = packed.astype(jnp.bfloat16)


def first_kernel(
    counts_ref, blocks_ref, offsets_ref, q_hbm, k_hbm, v_hbm, part_ref, k_ref, v_ref,
    q_ref, q_sem, sems, *work,
):
    fetch = pltpu.make_async_copy(q_hbm, q_ref, q_sem)
    fetch.start()
    member = lax.axis_index("blk")
    slots = k_ref.shape[0]
    tiles = (counts_ref[member] + tile_blocks - 1) // tile_blocks

    sides = ((k_hbm, k_ref), (v_hbm, v_ref))

    def copy_of(side, tile):
        here = pl.ds(tile * tile_blocks, tile_blocks)
        source, target = sides[side]
        return pltpu.make_async_copy(source.at[here], target.at[here], sems.at[side, tile])

    for side in range(2):
        for tile in range(slots // tile_blocks):

            @pl.when(tile < tiles)
            def _():
                copy_of(side, tile).start()

    fetch.wait()

    def ready(tile):
        for side in range(2):
            copy_of(side, tile).wait()

    attend_rows(
        [member], counts_ref, blocks_ref, offsets_ref, [q_ref], k_ref, v_ref, [part_ref],
        *work, ready,
    )


def next_kernel(bits, counts_ref, blocks_ref, offsets_ref, k_ref, v_ref, *refs):
    n = len(bits)
    member = lax.axis_index("blk")
    attend_rows(
        [jnp.bitwise_xor(member, bit) for bit in bits],
        counts_ref, blocks_ref, offsets_ref, refs[:n], k_ref, v_ref, refs[n : 2 * n],
        *refs[2 * n :], lambda tile: None,
    )


def attend(bits, queries, keys, values, tables):
    n = len(bits)
    rows, width = queries[0].shape
    slots, block_len, _ = keys.shape
    tiles = slots // tile_blocks
    smem = pl.BlockSpec(memory_space=pltpu.SMEM)
    vmem = pl.BlockSpec(memory_space=pltpu.VMEM)
    hbm = pl.BlockSpec(memory_space=pltpu.HBM)
    part = jax.ShapeDtypeStruct((rows + stat_rows, width), jnp.bfloat16)
    work = [
        pltpu.VMEM((tiles, tile_blocks, n * rows, block_len), jnp.float32),
        pltpu.VMEM((n * rows, lanes), jnp.int32),
        pltpu.VMEM((n * rows, 2 * width), jnp.bfloat16),
    ]
    used = 4 * n * rows * slots * block_len + 2**21
    kept = 5 * slots * block_len * width
    common = dict(
        cost_estimate=pl.CostEstimate(
            flops=4 * n * rows * width * slots * block_len,
            bytes_accessed=4 * slots * block_len * width,
            transcendentals=n * rows * slots * block_len,
        ),
        name="attend_" + "_".join(str(bit) for bit in bits),
    )
    if bits == (0,):
        return pl.pallas_call(
            first_kernel,
            out_shape=[part, keys, values],
            in_specs=[smem] * 3 + [hbm] * 3,
            out_specs=[vmem] * 3,
            scratch_shapes=[
                pltpu.VMEM((rows, width), jnp.bfloat16),
                pltpu.SemaphoreType.DMA,
                pltpu.SemaphoreType.DMA((2, tiles)),
            ]
            + work,
            compiler_params=pltpu.CompilerParams(vmem_limit_bytes=used + kept),
            **common,
        )(*tables, *(pltpu.with_memory_space_constraint(x, pltpu.HBM) for x in (*queries, keys, values)))
    return pl.pallas_call(
        functools.partial(next_kernel, bits),
        out_shape=[part] * n,
        in_specs=[smem] * 3 + [vmem] * (n + 2),
        out_specs=[vmem] * n,
        scratch_shapes=work,
        compiler_params=pltpu.CompilerParams(vmem_limit_bytes=used),
        **common,
    )(*tables, keys, values, *queries)


def merge_kernel(*refs):
    parts, out_ref = refs[:-1], refs[-1]
    rows, width = out_ref.shape
    levels = []
    for part in parts:
        stats = part[rows:, :].astype(jnp.float32)
        levels.append(stats[0:1] + stats[1:2] + stats[2:3])
    top = functools.reduce(jnp.maximum, levels)
    weights = [jnp.exp2(level - top) for level in levels]
    total = functools.reduce(lambda a, b: a + b, weights)
    summed = jnp.zeros((rows, width), jnp.float32)
    for part, weight in zip(parts, weights):
        column = jnp.transpose(jnp.broadcast_to(weight / total, (width, rows)))
        summed = summed + column * part[:rows, :].astype(jnp.float32)
    out_ref[...] = summed.astype(jnp.bfloat16)


def merge(parts, rows, width):
    vmem = pl.BlockSpec(memory_space=pltpu.VMEM)
    return pl.pallas_call(
        merge_kernel,
        out_shape=jax.ShapeDtypeStruct((rows, width), jnp.bfloat16),
        in_specs=[vmem] * len(parts),
        out_specs=vmem,
        compiler_params=pltpu.CompilerParams(vmem_limit_bytes=2**21),
        name="merge",
    )(*parts)


def swapped(x, bit):
    return lax.ppermute(x, "blk", [(i, i ^ bit) for i in range(lax.axis_size("blk"))])


def per_device(queries, key_cache, cached_value_slots, block_counts, slot_blocks, offsets):
    tokens, heads, width = queries.shape
    members = lax.axis_size("blk")
    own = queries.reshape(tokens * heads, width)
    tables = (block_counts, slot_blocks, offsets)
    held = {bit: swapped(own, bit) for bit in range(1, members)}
    part, keys, values = attend((0,), [own], key_cache[0], cached_value_slots[0], tables)
    parts = [part]
    bits = tuple(range(1, members))
    for start in range(0, len(bits), group_parts):
        some = bits[start : start + group_parts]
        fresh = attend(some, [held[bit] for bit in some], keys, values, tables)
        parts += [swapped(x, bit) for x, bit in zip(fresh, some)]
    return merge(parts, tokens * heads, width).reshape(tokens, heads, width)


def solution(mesh):
    in_specs = (
        P(("groups", "blk"), ("head", "sub"), None),
        P("head", ("groups", "blk"), None, None),
        P("head", ("groups", "blk"), None, None),
        P("groups"),
        P("groups"),
        P("groups"),
    )
    out_specs = P(("groups", "blk"), ("head", "sub"), None)
    return jax.shard_map(
        per_device, mesh=mesh, in_specs=in_specs, out_specs=out_specs, check_vma=False
    )
```

```python
import functools

import jax
import jax.numpy as jnp
from jax import lax
from jax.experimental import pallas as pl
from jax.experimental.pallas import tpu as pltpu
from jax.sharding import PartitionSpec as P

masked_score = -1e30
lowest_max = -1e29
lanes = 128
group = 8
stat_rows = 16
tile_blocks = 8
together = 1
log2_e = 1.4426950408889634
far = 2**30


def split_three(x):
    high = x.astype(jnp.bfloat16)
    rest = x - high.astype(jnp.float32)
    middle = rest.astype(jnp.bfloat16)
    low = (rest - middle.astype(jnp.float32)).astype(jnp.bfloat16)
    return high.astype(jnp.float32), middle.astype(jnp.float32), low.astype(jnp.float32)


def in_vmem():
    return pl.BlockSpec(memory_space=pltpu.VMEM)


def fetch_kernel(
    counts_hbm, blocks_hbm, offsets_hbm, q_hbm, k_hbm, v_hbm,
    q_ref, k_ref, v_ref, first_ref, room_ref,
    counts_ref, blocks_ref, offsets_ref, sems,
):
    pairs = (
        (counts_hbm, counts_ref),
        (blocks_hbm, blocks_ref),
        (offsets_hbm, offsets_ref),
        (k_hbm, k_ref),
        (v_hbm, v_ref),
        (q_hbm, q_ref),
    )
    copies = [
        pltpu.make_async_copy(source, target, sems.at[i])
        for i, (source, target) in enumerate(pairs)
    ]
    for copy in copies:
        copy.start()
    for copy in copies[:3]:
        copy.wait()
    members = lax.axis_size("blk")
    member = lax.axis_index("blk")
    slots, block_len, _ = k_ref.shape
    tokens = offsets_ref.shape[0] // members
    per_token = room_ref.shape[1] // tokens
    count = counts_ref[member]
    for slot in range(slots):
        block = blocks_ref[member * slots + slot]
        first = jnp.where(slot < count, block * block_len, far)
        first_ref[slot] = jnp.full((group, lanes), first, jnp.int32)
    first_ref[slots] = jnp.full((group, lanes), count, jnp.int32)
    lane = lax.broadcasted_iota(jnp.int32, (group, lanes), 1)
    for bit in range(members):
        home = jnp.bitwise_xor(member, bit)
        for t in range(tokens):
            room = offsets_ref[home * tokens + t] - lane
            for i in range(per_token):
                room_ref[bit, t * per_token + i] = room
    for copy in copies[3:]:
        copy.wait()


def fetch(queries, keys, values, tables):
    rows, width = queries.shape
    slots, block_len, _ = keys.shape
    members = lax.axis_size("blk")
    rooms = (members, rows // group, group, lanes)
    given = [pltpu.with_memory_space_constraint(x, pltpu.HBM) for x in (*tables, queries, keys, values)]
    hbm = pl.BlockSpec(memory_space=pltpu.HBM)
    return pl.pallas_call(
        fetch_kernel,
        out_shape=[
            queries,
            keys,
            values,
            jax.ShapeDtypeStruct((slots + 1, group, lanes), jnp.int32),
            jax.ShapeDtypeStruct(rooms, jnp.int32),
        ],
        in_specs=[hbm] * 6,
        out_specs=[in_vmem()] * 5,
        scratch_shapes=[pltpu.SMEM(x.shape, jnp.int32) for x in tables]
        + [pltpu.SemaphoreType.DMA((6,))],
        compiler_params=pltpu.CompilerParams(
            vmem_limit_bytes=4 * slots * block_len * width + 4 * members * rows * lanes + 2**20
        ),
        name="fetch",
    )(*given)


def attend_kernel(bits, first_ref, room_ref, k_ref, v_ref, *refs):
    n = len(bits)
    q_refs, part_refs = refs[:n], refs[n : 2 * n]
    score_ref, q_ref = refs[2 * n :]
    rows, width = q_refs[0].shape
    slots, block_len, _ = k_ref.shape
    every = n * rows
    tiles = (jnp.max(first_ref[slots]) + tile_blocks - 1) // tile_blocks
    scale = width ** (-0.5) * log2_e
    acc_shape = (every, 2 * width)

    for part in range(n):
        here = slice(part * rows, (part + 1) * rows)
        scaled = q_refs[part][...].astype(jnp.float32) * scale
        high = scaled.astype(jnp.bfloat16)
        q_ref[here, :width] = high
        q_ref[here, width:] = (scaled - high.astype(jnp.float32)).astype(jnp.bfloat16)
    rooms = [room_ref[bit] for bit in bits]
    room = rooms[0] if n == 1 else jnp.concatenate(rooms, axis=0)

    def score_pass(accs):
        def score_tile(tile, top):
            for i in range(tile_blocks):
                keys = k_ref[tile * tile_blocks + i]
                stage = (i // 2) % 2
                pltpu.matmul_push_rhs(
                    jnp.concatenate([keys, keys], axis=1), stage, i % 2, transpose=True
                )
                pltpu.matmul_acc_lhs(accs[i], q_ref[...], stage)
            for i in range(tile_blocks):
                first = first_ref[tile * tile_blocks + i]
                s = pltpu.matmul_pop(accs[i])
                for c in range(0, block_len, lanes):
                    piece = s[:, c : c + lanes].reshape(every // group, group, lanes)
                    piece = jnp.where(room > (first + c)[None], piece, masked_score)
                    score_ref[tile, i, c // lanes] = piece
                    top = jnp.maximum(top, piece)
            return top

        start = jnp.full((every // group, group, lanes), lowest_max, jnp.float32)
        return lax.fori_loop(0, tiles, score_tile, start)

    top = pl.run_scoped(
        score_pass, [pltpu.ACC(i % 2)(acc_shape, jnp.float32) for i in range(tile_blocks)]
    )
    top = jnp.broadcast_to(jnp.max(top, axis=2, keepdims=True), top.shape)
    ones = jnp.ones((block_len, lanes), jnp.bfloat16)

    def value_pass(accs):
        def value_tile(tile, carried):
            for i in range(tile_blocks):
                values = v_ref[tile * tile_blocks + i]
                stage = (i // 2) % 2
                pltpu.matmul_push_rhs(jnp.concatenate([values, ones], axis=1), stage, i % 2)
                weights = [
                    jnp.exp2(score_ref[tile, i, c] - top).reshape(every, lanes).astype(jnp.bfloat16)
                    for c in range(block_len // lanes)
                ]
                pltpu.matmul_acc_lhs(accs[i % 2], jnp.concatenate(weights, axis=1), stage)
            return carried

        lax.fori_loop(0, tiles, value_tile, 0)
        return pltpu.matmul_pop(accs[0]) + pltpu.matmul_pop(accs[1])

    both = pl.run_scoped(value_pass, [pltpu.ACC(i)(acc_shape, jnp.float32) for i in range(2)])
    total = both[:, width:]
    empty = total <= 0.0
    safe = jnp.where(empty, 1.0, total)
    level = jnp.where(empty, masked_score, top.reshape(every, lanes) + jnp.log2(safe))
    summed = both[:, :width] / safe
    for part, part_ref in enumerate(part_refs):
        here = slice(part * rows, (part + 1) * rows)
        part_ref[:rows, :] = summed[here].astype(jnp.bfloat16)
        levels = jnp.transpose(level[here])[:stat_rows]
        high, middle, low = split_three(levels)
        row = lax.broadcasted_iota(jnp.int32, levels.shape, 0)
        packed = jnp.where(row == 0, high, jnp.where(row == 1, middle, low))
        part_ref[rows:, :] = packed.astype(jnp.bfloat16)


def attend(bits, queries, cache):
    keys, values, firsts, rooms = cache
    n = len(bits)
    rows, width = queries[0].shape
    slots, block_len, _ = keys.shape
    tiles = slots // tile_blocks
    part = jax.ShapeDtypeStruct((rows + stat_rows, width), jnp.bfloat16)
    scores = (tiles, tile_blocks, block_len // lanes, n * rows // group, group, lanes)
    return pl.pallas_call(
        functools.partial(attend_kernel, bits),
        out_shape=[part] * n,
        in_specs=[in_vmem()] * (n + 4),
        out_specs=[in_vmem()] * n,
        scratch_shapes=[
            pltpu.VMEM(scores, jnp.float32),
            pltpu.VMEM((n * rows, 2 * width), jnp.bfloat16),
        ],
        compiler_params=pltpu.CompilerParams(
            vmem_limit_bytes=4 * n * rows * slots * block_len + 2**21
        ),
        cost_estimate=pl.CostEstimate(
            flops=4 * n * rows * width * slots * block_len,
            bytes_accessed=4 * slots * block_len * width,
            transcendentals=n * rows * slots * block_len,
        ),
        name="attend_" + "_".join(str(bit) for bit in bits),
    )(firsts, rooms, keys, values, *queries)


def merge_kernel(*refs):
    parts, out_ref = refs[:-1], refs[-1]
    rows, width = out_ref.shape
    levels = []
    for part in parts:
        stats = part[rows:, :].astype(jnp.float32)
        levels.append(stats[0:1] + stats[1:2] + stats[2:3])
    top = functools.reduce(jnp.maximum, levels)
    weights = [jnp.exp2(level - top) for level in levels]
    total = functools.reduce(lambda a, b: a + b, weights)
    summed = jnp.zeros((rows, width), jnp.float32)
    for part, weight in zip(parts, weights):
        column = jnp.transpose(jnp.broadcast_to(weight / total, (width, rows)))
        summed = summed + column * part[:rows, :].astype(jnp.float32)
    out_ref[...] = summed.astype(jnp.bfloat16)


def merge(parts, rows, width):
    return pl.pallas_call(
        merge_kernel,
        out_shape=jax.ShapeDtypeStruct((rows, width), jnp.bfloat16),
        in_specs=[in_vmem()] * len(parts),
        out_specs=in_vmem(),
        compiler_params=pltpu.CompilerParams(vmem_limit_bytes=2**21),
        name="merge",
    )(*parts)


def swapped(x, bit):
    return lax.ppermute(x, "blk", [(i, i ^ bit) for i in range(lax.axis_size("blk"))])


def per_device(queries, key_cache, cached_value_slots, block_counts, slot_blocks, offsets):
    tokens, heads, width = queries.shape
    members = lax.axis_size("blk")
    own = queries.reshape(tokens * heads, width)
    bits = tuple(range(members - 1, 0, -1))
    held = {bit: swapped(own, bit) for bit in bits}
    held[0], *cache = fetch(
        own, key_cache[0], cached_value_slots[0], (block_counts, slot_blocks, offsets)
    )
    parts = []
    for start in range(0, len(bits), together):
        some = bits[start : start + together]
        fresh = attend(some, [held[bit] for bit in some], cache)
        parts += [swapped(x, bit) for x, bit in zip(fresh, some)]
    parts += attend((0,), [held[0]], cache)
    return merge(parts, tokens * heads, width).reshape(tokens, heads, width)


def solution(mesh):
    in_specs = (
        P(("groups", "blk"), ("head", "sub"), None),
        P("head", ("groups", "blk"), None, None),
        P("head", ("groups", "blk"), None, None),
        P("groups"),
        P("groups"),
        P("groups"),
    )
    out_specs = P(("groups", "blk"), ("head", "sub"), None)
    return jax.shard_map(
        per_device, mesh=mesh, in_specs=in_specs, out_specs=out_specs, check_vma=False
    )
```
